32 devices in a mesh: seq: 8 (over z, y), head: 4 (over x, core).
Axes of the slice: x: 2, y: 2, z: 4, core: 2. Of those that a mesh axis runs over, the one named last changes fastest.
Arguments:
- queries: bfloat16 [4096, 2048], P('seq', 'head'), may hold values from -8 to 8
- keys: bfloat16 [4096, 1024], P('seq', 'head'), may hold values from -8 to 8
- values: bfloat16 [4096, 1024], P('seq', 'head'), may hold values from -6 to 6
- output_gradient: bfloat16 [4096, 2048], P('seq', 'head'), may hold values from -6 to 6
- key_exponents: int32 [32, 8], P('seq', 'head'), may hold values from -1 to 1
- value_exponents: int32 [32, 8], P('seq', 'head'), may hold values from -1 to 1
- key_matrix: bfloat16 [5376, 1024], P(None, 'head'), may hold values from -0.1875 to 0.1875
- value_matrix: bfloat16 [5376, 1024], P(None, 'head'), may hold values from -0.1875 to 0.1875
Outputs:
- query_grad: bfloat16 [4096, 2048], P('seq', 'head')
- input_grad: bfloat16 [5376, 4096], P('head', 'seq')
The draws below stay inside these ranges and needn't reach their ends.
All inputs are finite; a program needn't handle non-finite values.
Results may differ from the reference program's by a relative error of at most 0.015.
Values may be sent and summed in bfloat16 or wider, within the bound.
A program may use at most 64 MiB of HBM per device.

```python
import math
import jax
import jax.numpy as jnp
from jax import lax

MODEL_WIDTH = 5376
QUERY_HEADS = 16
KEY_VALUE_HEADS = 8
HEAD_SIZE = 128
QUERY_SCALE = 168
ATTEND_WINDOW = 1024
SCALE_BLOCK = 128
SEQUENCE_TOKENS = 4096
N_HEAD = 4


def draw_queries(key, part):
    window_entries = jax.random.normal(jax.random.fold_in(key, 5), (SEQUENCE_TOKENS, QUERY_HEADS, HEAD_SIZE), jnp.float32)
    return jnp.clip(window_entries, -8.0, 8.0).reshape(SEQUENCE_TOKENS, QUERY_HEADS * HEAD_SIZE).astype(jnp.bfloat16)


def draw_keys(key, part):
    window_offsets = jax.random.normal(jax.random.fold_in(key, 7), (SEQUENCE_TOKENS // SCALE_BLOCK, KEY_VALUE_HEADS, HEAD_SIZE), jnp.float32)
    window_offsets = jnp.repeat(window_offsets, SCALE_BLOCK, axis=0)
    window_entries = jax.random.normal(jax.random.fold_in(key, 6), (SEQUENCE_TOKENS, KEY_VALUE_HEADS, HEAD_SIZE), jnp.float32) + window_offsets
    return jnp.clip(window_entries, -8.0, 8.0).reshape(SEQUENCE_TOKENS, KEY_VALUE_HEADS * HEAD_SIZE).astype(jnp.bfloat16)


def place_ends(values, stream_key, low, top_value):
    longest = values.shape.index(max(values.shape))
    spots = []
    for shift in (0, 1):
        where = [jax.random.randint(jax.random.fold_in(stream_key, axis), (), 0, length) for axis, length in enumerate(values.shape)]
        where[longest] = (where[longest] + shift) % values.shape[longest]
        spots.append(tuple(where))
    return values.at[spots[0]].set(low).at[spots[1]].set(top_value)


def level_of(key, dims, shards, low, top_value):
    def one(axis_at, shards_of):
        heights = jax.random.uniform(jax.random.fold_in(jax.random.fold_in(key, 6), axis_at), (shards_of,), jnp.float32, low / len(shards), top_value / len(shards))
        return jnp.repeat(jnp.exp(heights), dims[axis_at] // shards_of).reshape((-1,) + (1,) * (len(dims) - axis_at - 1))

    gain = one(*shards[0])
    for cut in shards[1:]:
        gain = gain * one(*cut)
    return gain


def centred(key, extent, scale, most, cuts=(), kind=jnp.bfloat16):
    entries = jax.random.normal(key, extent, jnp.float32) * scale
    if len(cuts) > 0:
        entries = level_of(key, extent, cuts, -0.22, 0.18) * entries
    return jnp.clip(entries, min=-most, max=most).astype(kind)


def setup_inputs(seed: int = 0) -> dict:
    arg_keys = jax.random.split(jax.random.key(seed), 9)
    return {
        "queries": draw_queries(jax.random.fold_in(arg_keys[8], 71), 0),
        "keys": draw_keys(jax.random.fold_in(arg_keys[8], 71), 0),
        "values": centred(arg_keys[2], (SEQUENCE_TOKENS, KEY_VALUE_HEADS * HEAD_SIZE), 1.0, 6.0, ((0, 8), (1, 4))),
        "output_gradient": centred(arg_keys[3], (SEQUENCE_TOKENS, QUERY_HEADS * HEAD_SIZE), 1.0, 6.0, ((0, 8), (1, 4))),
        "key_exponents": place_ends(jax.random.randint(arg_keys[4], (SEQUENCE_TOKENS // SCALE_BLOCK, KEY_VALUE_HEADS), -1, 2), jax.random.fold_in(arg_keys[4], 1), -1, 1).astype(jnp.int32),
        "value_exponents": place_ends(jax.random.randint(arg_keys[5], (SEQUENCE_TOKENS // SCALE_BLOCK, KEY_VALUE_HEADS), -1, 2), jax.random.fold_in(arg_keys[5], 1), -1, 1).astype(jnp.int32),
        "key_matrix": centred(arg_keys[6], (MODEL_WIDTH, KEY_VALUE_HEADS * HEAD_SIZE), (KEY_VALUE_HEADS * HEAD_SIZE) ** -0.5, 0.1875, ((1, 4),)),
        "value_matrix": centred(arg_keys[7], (MODEL_WIDTH, KEY_VALUE_HEADS * HEAD_SIZE), (KEY_VALUE_HEADS * HEAD_SIZE) ** -0.5, 0.1875, ((1, 4),)),
    }


def power_of_two(exponents):
    return jnp.where(exponents > 0, 2.0, jnp.where(exponents < 0, 0.5, 1.0)).astype(jnp.float32)


def reference(queries, keys, values, output_gradient, key_exponents, value_exponents, key_matrix, value_matrix):
    score_scale = QUERY_SCALE ** -0.5
    group_width = QUERY_HEADS // KEY_VALUE_HEADS
    key_multiplier = jnp.repeat(power_of_two(key_exponents), SCALE_BLOCK, axis=0)[:, :, None]
    value_multiplier = jnp.repeat(power_of_two(value_exponents), SCALE_BLOCK, axis=0)[:, :, None]
    exact_keys = (keys.astype(jnp.float32).reshape(SEQUENCE_TOKENS, KEY_VALUE_HEADS, HEAD_SIZE) * key_multiplier).astype(jnp.bfloat16)
    exact_values = (values.astype(jnp.float32).reshape(SEQUENCE_TOKENS, KEY_VALUE_HEADS, HEAD_SIZE) * value_multiplier).astype(jnp.bfloat16)
    running_sum = jnp.cumsum(exact_keys.astype(jnp.float32), axis=0)
    preceding = jnp.concatenate([jnp.zeros((ATTEND_WINDOW, KEY_VALUE_HEADS, HEAD_SIZE), jnp.float32), running_sum], 0)[:SEQUENCE_TOKENS]
    places = jnp.arange(SEQUENCE_TOKENS, dtype=jnp.int32)
    counts = jnp.minimum(places + 1, ATTEND_WINDOW).astype(jnp.float32)
    key_mean = (running_sum - preceding) / counts[:, None, None]
    smoothed_keys = (exact_keys.astype(jnp.float32) - key_mean).astype(jnp.bfloat16)

    block_rows = math.gcd(SEQUENCE_TOKENS, 512)
    key_padding = jnp.concatenate([jnp.zeros((ATTEND_WINDOW, KEY_VALUE_HEADS, HEAD_SIZE), jnp.bfloat16), smoothed_keys], 0)
    value_padding = jnp.concatenate([jnp.zeros((ATTEND_WINDOW, KEY_VALUE_HEADS, HEAD_SIZE), jnp.bfloat16), exact_values], 0)
    query_head_count = queries.reshape(SEQUENCE_TOKENS, KEY_VALUE_HEADS, group_width, HEAD_SIZE)
    gradient_heads = output_gradient.reshape(SEQUENCE_TOKENS, KEY_VALUE_HEADS, group_width, HEAD_SIZE)

    def one_block(block_index):
        begin_row = block_index * block_rows
        query_rows = lax.dynamic_slice_in_dim(query_head_count, begin_row, block_rows, 0).astype(jnp.float32)
        grad_rows = lax.dynamic_slice_in_dim(gradient_heads, begin_row, block_rows, 0).astype(jnp.float32)
        key_rows = lax.dynamic_slice_in_dim(key_padding, begin_row, block_rows + ATTEND_WINDOW, 0).astype(jnp.float32)
        value_rows = lax.dynamic_slice_in_dim(value_padding, begin_row, block_rows + ATTEND_WINDOW, 0).astype(jnp.float32)
        query_at = begin_row + jnp.arange(block_rows, dtype=jnp.int32)
        key_at = begin_row - ATTEND_WINDOW + jnp.arange(block_rows + ATTEND_WINDOW, dtype=jnp.int32)
        distance = query_at[:, None] - key_at[None, :]
        allowed = (distance >= 0) & (distance < ATTEND_WINDOW) & (key_at[None, :] >= 0)
        scores = jnp.einsum("qhgd,khd->hgqk", query_rows, key_rows) * score_scale
        scores = jnp.where(allowed, scores, -jnp.inf)
        highest = jnp.max(scores, axis=-1, keepdims=True)
        weights = jnp.exp(scores - highest)
        shares = weights / jnp.sum(weights, axis=-1, keepdims=True)
        rounded = lax.optimization_barrier(shares.astype(jnp.bfloat16)).astype(jnp.float32)
        attended = jnp.einsum("hgqk,khd->hgqd", rounded, value_rows)
        row_dot = jnp.einsum("hgqd,qhgd->hgq", attended, grad_rows)[..., None]
        share_grad = jnp.einsum("qhgd,khd->hgqk", grad_rows, value_rows)
        score_grad = lax.optimization_barrier((shares * (share_grad - row_dot)).astype(jnp.bfloat16)).astype(jnp.float32)
        query_part = (score_scale * jnp.einsum("hgqk,khd->qhgd", score_grad, key_rows)).astype(jnp.bfloat16)
        key_part = score_scale * jnp.einsum("hgqk,qhgd->khd", score_grad, query_rows)
        value_part = jnp.einsum("hgqk,qhgd->khd", rounded, grad_rows)
        return query_part, key_part, value_part

    def advance(carried, block_index):
        key_gradient_sum, value_gradient_sum = carried
        query_part, key_part, value_part = one_block(block_index)
        begin_row = block_index * block_rows
        key_gradient_sum = lax.dynamic_update_slice_in_dim(
            key_gradient_sum, lax.dynamic_slice_in_dim(key_gradient_sum, begin_row, block_rows + ATTEND_WINDOW, 0) + key_part, begin_row, 0)
        value_gradient_sum = lax.dynamic_update_slice_in_dim(
            value_gradient_sum, lax.dynamic_slice_in_dim(value_gradient_sum, begin_row, block_rows + ATTEND_WINDOW, 0) + value_part, begin_row, 0)
        return (key_gradient_sum, value_gradient_sum), query_part

    blank_rows = jnp.zeros((SEQUENCE_TOKENS + ATTEND_WINDOW, KEY_VALUE_HEADS, HEAD_SIZE), jnp.float32)
    (key_gradient_sum, value_gradient_sum), query_parts = lax.scan(
        advance, (blank_rows, blank_rows), jnp.arange(SEQUENCE_TOKENS // block_rows, dtype=jnp.int32))
    query_grad = query_parts.reshape(SEQUENCE_TOKENS, QUERY_HEADS * HEAD_SIZE)
    scaled_keys = (key_gradient_sum[ATTEND_WINDOW:] * key_multiplier).astype(jnp.bfloat16).reshape(SEQUENCE_TOKENS, KEY_VALUE_HEADS * HEAD_SIZE)
    scaled_values = (value_gradient_sum[ATTEND_WINDOW:] * value_multiplier).astype(jnp.bfloat16).reshape(SEQUENCE_TOKENS, KEY_VALUE_HEADS * HEAD_SIZE)

    group_members = KEY_VALUE_HEADS * HEAD_SIZE // N_HEAD
    summed = jnp.zeros((MODEL_WIDTH, SEQUENCE_TOKENS), jnp.float32)
    for group_index in range(N_HEAD):
        first_col = group_index * group_members
        last_col = first_col + group_members
        partial_value = jnp.dot(key_matrix[:, first_col:last_col], scaled_keys[:, first_col:last_col].T,
                          preferred_element_type=jnp.float32)
        partial_value = partial_value + jnp.dot(value_matrix[:, first_col:last_col], scaled_values[:, first_col:last_col].T,
                                    preferred_element_type=jnp.float32)
        summed = summed + lax.optimization_barrier(partial_value.astype(jnp.bfloat16)).astype(jnp.float32)
    return query_grad, summed.astype(jnp.bfloat16)
```

```python
import functools

import jax
import jax.numpy as jnp
from jax import lax
from jax.experimental import pallas as pl
from jax.experimental.pallas import tpu as pltpu
from jax.sharding import PartitionSpec as P

HEAD_SIZE = 128
QUERY_SCALE = 168
ATTEND_WINDOW = 1024
SCALE_BLOCK = 128
LOG2_E = 1.4426950408889634
MESH = pl.DeviceIdType.MESH
F32 = jnp.float32
BF16 = jnp.bfloat16


def power_of_two(exponent):
    return jnp.where(exponent > 0, 2.0, jnp.where(exponent < 0, 0.5, 1.0)).astype(F32)


def contract_last(a, b):
    return lax.dot_general(a, b, (((1,), (1,)), ((), ())), preferred_element_type=F32)


def partner(h, t):
    other, bit = h, 1
    while bit <= t:
        if t & bit:
            other = other + bit - 2 * bit * lax.rem(lax.div(h, bit), 2)
        bit *= 2
    return other


def kernel(
    n, nh, q_ref, k_ref, v_ref, do_ref, ke_ref, ve_ref, wk_ref, wv_ref, dq_ref, out_ref,
    key_true, raw_far, total_own, total_near, smooth, value, smooth_t, dk, dv, grad_out, grad_in,
    scaled, gathered, weights, acc,
    fwd_send, fwd_recv, w_send, w_recv, w_own, g_send, g_recv, s_send, s_recv,
):
    tokens = q_ref.shape[0]
    heads = k_ref.shape[1] // HEAD_SIZE
    D = HEAD_SIZE
    b = lax.axis_index("seq")
    h = lax.axis_index("head")
    rows = out_ref.shape[0]
    own = 2 * tokens

    def cols(g):
        return slice(g * D, (g + 1) * D)

    barrier = pltpu.get_barrier_semaphore()
    for d in (1, 2):
        for to in (lax.rem(b + d, n), lax.rem(b + n - d, n)):
            pl.semaphore_signal(barrier, inc=1, device_id={"seq": to}, device_id_type=MESH)
    for t in range(1, nh):
        pl.semaphore_signal(barrier, inc=1, device_id={"head": partner(h, t)}, device_id_type=MESH)
    pl.semaphore_wait(barrier, 4 + nh - 1)

    def along(src, dst, send, recv, step):
        return pltpu.make_async_remote_copy(
            src_ref=src, dst_ref=dst, send_sem=send, recv_sem=recv,
            device_id={"seq": lax.rem(b + n + step, n)}, device_id_type=MESH,
        )

    def across(src, dst, send, recv, t):
        return pltpu.make_async_remote_copy(
            src_ref=src, dst_ref=dst, send_sem=send, recv_sem=recv,
            device_id={"head": partner(h, t)}, device_id_type=MESH,
        )

    def when_start(condition, copies):
        @pl.when(condition)
        def _():
            for copy in copies:
                copy.start()

    weight_copies = []
    for t in list(range(2, nh)) + [1]:
        to = partner(h, t)
        for m, ref in enumerate((wk_ref, wv_ref)):
            copy = across(
                ref.at[pl.ds(to * rows, rows), :], weights.at[t, m],
                w_send.at[t, m], w_recv.at[t, m], t,
            )
            copy.start()
            weight_copies.append((t, copy))
    own_copies = []
    for m, ref in enumerate((wk_ref, wv_ref)):
        copy = pltpu.make_async_copy(ref.at[pl.ds(h * rows, rows), :], weights.at[0, m], w_own.at[m])
        copy.start()
        own_copies.append(copy)

    for j in range(tokens // SCALE_BLOCK):
        at = slice(j * SCALE_BLOCK, (j + 1) * SCALE_BLOCK)
        for g in range(heads):
            key_true[at, cols(g)] = (
                k_ref[at, cols(g)].astype(F32) * power_of_two(ke_ref[j, g])
            ).astype(BF16)
    key_far = along(key_true, raw_far, fwd_send.at[0], fwd_recv.at[0], 2)
    when_start(b + 2 < n, [key_far])
    keys_own = key_true[...]
    total_own[...] = jnp.broadcast_to(
        jnp.sum(keys_own.astype(F32), axis=0, keepdims=True), total_own.shape
    )
    sum_near = along(total_own, total_near, fwd_send.at[1], fwd_recv.at[1], 1)
    when_start(b + 1 < n, [sum_near])
    for j in range(tokens // SCALE_BLOCK):
        at = slice(j * SCALE_BLOCK, (j + 1) * SCALE_BLOCK)
        for g in range(heads):
            value[own + j * SCALE_BLOCK : own + (j + 1) * SCALE_BLOCK, cols(g)] = (
                v_ref[at, cols(g)].astype(F32) * power_of_two(ve_ref[j, g])
            ).astype(BF16)
    value_near = along(
        value.at[own : own + tokens], value.at[tokens:own], fwd_send.at[2], fwd_recv.at[2], 1
    )
    value_far = along(
        value.at[own : own + tokens], value.at[0:tokens], fwd_send.at[3], fwd_recv.at[3], 2
    )
    when_start(b + 1 < n, [value_near])
    when_start(b + 2 < n, [value_far])

    @pl.when(b < 1)
    def _():
        total_near[...] = jnp.zeros_like(total_near)
        value[tokens:own, :] = jnp.zeros((tokens, value.shape[1]), BF16)
        smooth[tokens:own, :] = jnp.zeros((tokens, value.shape[1]), BF16)

    @pl.when(b < 2)
    def _():
        raw_far[...] = jnp.zeros_like(raw_far)
        value[0:tokens, :] = jnp.zeros((tokens, value.shape[1]), BF16)
        smooth[0:tokens, :] = jnp.zeros((tokens, value.shape[1]), BF16)

    row_at = lax.broadcasted_iota(jnp.int32, (tokens, tokens), 0)
    col_at = lax.broadcasted_iota(jnp.int32, (tokens, tokens), 1)
    lower = jnp.where(row_at >= col_at, 1.0, 0.0).astype(BF16)
    running = jnp.dot(lower, keys_own, preferred_element_type=F32)
    place = b * tokens + lax.broadcasted_iota(jnp.int32, (tokens, 1), 0)
    counts = jnp.clip(place + 1, 1, ATTEND_WINDOW).astype(F32)

    @pl.when(b >= 1)
    def _():
        sum_near.wait_recv()

    @pl.when(b >= 2)
    def _():
        key_far.wait_recv()

    far = jnp.dot(lower, raw_far[...], preferred_element_type=F32)
    mean = (running - far + far[tokens - 1 :, :] + total_near[0:1, :]) / counts
    smooth[own : own + tokens, :] = (keys_own.astype(F32) - mean).astype(BF16)
    smooth_near = along(
        smooth.at[own : own + tokens], smooth.at[tokens:own], fwd_send.at[4], fwd_recv.at[4], 1
    )
    smooth_far = along(
        smooth.at[own : own + tokens], smooth.at[0:tokens], fwd_send.at[5], fwd_recv.at[5], 2
    )
    when_start(b + 1 < n, [smooth_near])
    when_start(b + 2 < n, [smooth_far])
    dk[...] = jnp.zeros_like(dk)
    dv[...] = jnp.zeros_like(dv)

    @pl.when(b >= 1)
    def _():
        value_near.wait_recv()
        smooth_near.wait_recv()

    @pl.when(b >= 2)
    def _():
        value_far.wait_recv()
        smooth_far.wait_recv()

    tile = SCALE_BLOCK
    span = ATTEND_WINDOW + tile
    scale = QUERY_SCALE ** (-0.5)
    group = q_ref.shape[1] // (heads * D)
    width = group * tile
    key_row = lax.broadcasted_iota(jnp.int32, (ATTEND_WINDOW, width), 0)
    near_row = lax.broadcasted_iota(jnp.int32, (tile, width), 0)
    lane = lax.rem(lax.broadcasted_iota(jnp.int32, (1, width), 1), tile)

    grad_copies = []
    for g in range(heads):
        smooth_t[...] = smooth[:, cols(g)].astype(F32).T.astype(BF16)

        def one_tile(i, carry, g=g):
            begin = pl.multiple_of(i * tile, tile)
            at = pl.ds(begin, tile)
            window = pl.ds(begin, span)
            q = jnp.concatenate([q_ref[at, cols(g * group + u)] for u in range(group)], 0)
            do = jnp.concatenate([do_ref[at, cols(g * group + u)] for u in range(group)], 0)
            keys = smooth[window, cols(g)]
            values = value[window, cols(g)]
            scores = contract_last(keys, q)
            first = jnp.maximum(lane + 1, (2 - b) * tokens - begin)
            scores = jnp.concatenate(
                [
                    jnp.where(key_row >= first, scores[:ATTEND_WINDOW], -jnp.inf),
                    jnp.where(near_row <= lane, scores[ATTEND_WINDOW:], -jnp.inf),
                ],
                0,
            )
            highest = jnp.max(scores, axis=0, keepdims=True)
            powers = jnp.exp2((scores - highest) * (scale * LOG2_E))
            shares = powers * (1.0 / jnp.sum(powers, axis=0, keepdims=True))
            rounded = shares.astype(BF16)
            share_grad = contract_last(values, do)
            row_dot = jnp.sum(rounded.astype(F32) * share_grad, axis=0, keepdims=True)
            score_grad = (shares * (share_grad - row_dot)).astype(BF16)
            dv[g, window, :] += jnp.dot(rounded, do, preferred_element_type=F32)
            dk[g, window, :] += jnp.dot(score_grad, q, preferred_element_type=F32)
            dq = jnp.dot(smooth_t[:, window], score_grad, preferred_element_type=F32) * scale
            dq = dq.T.astype(BF16)
            for u in range(group):
                dq_ref[at, cols(g * group + u)] = dq[u * tile : (u + 1) * tile]
            return carry

        lax.fori_loop(0, tokens // tile, one_tile, 0)
        for d in (2, 1):
            part = slice((2 - d) * tokens, (3 - d) * tokens)
            grad_out[g, d - 1, :, :D] = (dk[g, part, :] * scale).astype(BF16)
            grad_out[g, d - 1, :, D:] = dv[g, part, :].astype(BF16)
            copy = along(
                grad_out.at[g, d - 1], grad_in.at[g, d - 1],
                g_send.at[g, d - 1], g_recv.at[g, d - 1], -d,
            )
            when_start(b >= d, [copy])
            grad_copies.append((d, copy))

    share_copies = []
    for g in range(heads):
        for d in (1, 2):
            copy = grad_copies[g * 2 + (2 - d)][1]

            @pl.when(b + d < n)
            def _(copy=copy):
                copy.wait_recv()

            @pl.when(b + d >= n)
            def _(g=g, d=d):
                grad_in[g, d - 1] = jnp.zeros(grad_in.shape[2:], BF16)

        for j in range(tokens // SCALE_BLOCK):
            at = slice(j * SCALE_BLOCK, (j + 1) * SCALE_BLOCK)
            here = slice(own + j * SCALE_BLOCK, own + (j + 1) * SCALE_BLOCK)
            for m, (ref, exponent, factor) in enumerate(
                ((dk, ke_ref, scale), (dv, ve_ref, 1.0))
            ):
                whole = ref[g, here, :] * factor
                for d in (1, 2):
                    whole = whole + grad_in[g, d - 1, at, cols(m)].astype(F32)
                scaled[g, at, cols(m)] = (whole * power_of_two(exponent[j, g])).astype(BF16)
        for t in list(range(2, nh)) + [1]:
            copy = across(
                scaled.at[g], gathered.at[t - 1, g], s_send.at[t - 1, g], s_recv.at[t - 1, g], t
            )
            copy.start()
            share_copies.append((t, copy))

    chunk = rows // 4

    def product(t, at):
        total = None
        for g in range(heads):
            left = jnp.concatenate([weights[t, 0, at, cols(g)], weights[t, 1, at, cols(g)]], 1)
            right = scaled[g] if t == 0 else gathered[t - 1, g]
            term = contract_last(left, right)
            total = term if total is None else total + term
        return total

    for copy in own_copies:
        copy.wait()
    for t in range(nh):
        for source, copy in weight_copies + share_copies:
            if source == t:
                copy.wait_recv()

        def one_chunk(c, carry, t=t):
            at = pl.ds(pl.multiple_of(c * chunk, 16), chunk)
            total = product(t, at)
            if t > 0:
                total = total + acc[at, :]
            if t < nh - 1:
                acc[at, :] = total
            else:
                out_ref[at, :] = total.astype(BF16)
            return carry

        lax.fori_loop(0, 4, one_chunk, 0)

    @pl.when(b + 1 < n)
    def _():
        for copy in (sum_near, value_near, smooth_near):
            copy.wait_send()

    @pl.when(b + 2 < n)
    def _():
        for copy in (key_far, value_far, smooth_far):
            copy.wait_send()

    for d, copy in grad_copies:
        @pl.when(b >= d)
        def _(copy=copy):
            copy.wait_send()

    for _, copy in weight_copies + share_copies:
        copy.wait_send()


def solution(mesh):
    n, nh = mesh.shape["seq"], mesh.shape["head"]

    def local(q, k, v, do, ke, ve, wk, wv):
        tokens, width = k.shape
        heads = width // HEAD_SIZE
        assert ATTEND_WINDOW == 2 * tokens
        rows = wk.shape[0] // nh
        vmem = pl.BlockSpec(memory_space=pltpu.VMEM)
        smem = pl.BlockSpec(memory_space=pltpu.SMEM)
        hbm = pl.BlockSpec(memory_space=pl.ANY)
        dma = pltpu.SemaphoreType.DMA
        return pl.pallas_call(
            functools.partial(kernel, n, nh),
            out_shape=(
                jax.ShapeDtypeStruct(q.shape, BF16),
                jax.ShapeDtypeStruct((rows, tokens), BF16),
            ),
            in_specs=[vmem, vmem, vmem, vmem, smem, smem, hbm, hbm],
            out_specs=(vmem, vmem),
            scratch_shapes=[
                pltpu.VMEM((tokens, width), BF16),
                pltpu.VMEM((tokens, width), BF16),
                pltpu.VMEM((8, width), F32),
                pltpu.VMEM((8, width), F32),
                pltpu.VMEM((3 * tokens, width), BF16),
                pltpu.VMEM((3 * tokens, width), BF16),
                pltpu.VMEM((HEAD_SIZE, 3 * tokens), BF16),
                pltpu.VMEM((heads, 3 * tokens, HEAD_SIZE), F32),
                pltpu.VMEM((heads, 3 * tokens, HEAD_SIZE), F32),
                pltpu.VMEM((heads, 2, tokens, 2 * HEAD_SIZE), BF16),
                pltpu.VMEM((heads, 2, tokens, 2 * HEAD_SIZE), BF16),
                pltpu.VMEM((heads, tokens, 2 * HEAD_SIZE), BF16),
                pltpu.VMEM((nh - 1, heads, tokens, 2 * HEAD_SIZE), BF16),
                pltpu.VMEM((nh, 2, rows, width), BF16),
                pltpu.VMEM((rows, tokens), F32),
                dma((6,)), dma((6,)),
                dma((nh, 2)), dma((nh, 2)), dma((2,)),
                dma((heads, 2)), dma((heads, 2)),
                dma((nh - 1, heads)), dma((nh - 1, heads)),
            ],
            compiler_params=pltpu.CompilerParams(
                collective_id=0, has_side_effects=True, vmem_limit_bytes=56 * 2**20
            ),
        )(q, k, v, do, ke, ve, wk, wv)

    in_specs = (P("seq", "head"),) * 6 + (P(None, "head"),) * 2
    out_specs = (P("seq", "head"), P("head", "seq"))
    return jax.shard_map(local, mesh=mesh, in_specs=in_specs, out_specs=out_specs, check_vma=False)
```

```python
import functools

import jax
import jax.numpy as jnp
from jax import lax
from jax.experimental import pallas as pl
from jax.experimental.pallas import tpu as pltpu
from jax.sharding import PartitionSpec as P

HEAD_SIZE = 128
QUERY_SCALE = 168
ATTEND_WINDOW = 1024
SCALE_BLOCK = 128
LOG2_E = 1.4426950408889634
MESH = pl.DeviceIdType.MESH
F32 = jnp.float32
BF16 = jnp.bfloat16


def power_of_two(exponent):
    return jnp.where(exponent > 0, 2.0, jnp.where(exponent < 0, 0.5, 1.0)).astype(F32)


def contract_last(a, b):
    return lax.dot_general(a, b, (((1,), (1,)), ((), ())), preferred_element_type=F32)


def partner(h, t):
    other, bit = h, 1
    while bit <= t:
        if t & bit:
            other = other + bit - 2 * bit * lax.rem(lax.div(h, bit), 2)
        bit *= 2
    return other


def kernel(
    n, nh, q_ref, k_ref, v_ref, do_ref, ke_ref, ve_ref, wk_ref, wv_ref, dq_ref, out_ref,
    key_true, raw_far, total_own, total_near, smooth, value, smooth_t, dk, dv, grad_out, grad_in,
    scaled, gathered, weights, acc,
    fwd_send, fwd_recv, w_send, w_recv, y_send, y_recv, w_own, g_send, g_recv, far_send, far_recv, s_send, s_recv,
):
    tokens = q_ref.shape[0]
    heads = k_ref.shape[1] // HEAD_SIZE
    D = HEAD_SIZE
    b = lax.axis_index("seq")
    h = lax.axis_index("head")
    rows = out_ref.shape[0]
    own = 2 * tokens

    def cols(g):
        return slice(g * D, (g + 1) * D)

    barrier = pltpu.get_barrier_semaphore()
    for d in (1, 2):
        for to in (lax.rem(b + d, n), lax.rem(b + n - d, n)):
            pl.semaphore_signal(barrier, inc=1, device_id={"seq": to}, device_id_type=MESH)
    for t in range(1, nh):
        pl.semaphore_signal(barrier, inc=1, device_id={"head": partner(h, t)}, device_id_type=MESH)
    pl.semaphore_wait(barrier, 4 + nh - 1)

    def along(src, dst, send, recv, step):
        return pltpu.make_async_remote_copy(
            src_ref=src, dst_ref=dst, send_sem=send, recv_sem=recv,
            device_id={"seq": lax.rem(b + n + step, n)}, device_id_type=MESH,
        )

    def across(src, dst, send, recv, t):
        return pltpu.make_async_remote_copy(
            src_ref=src, dst_ref=dst, send_sem=send, recv_sem=recv,
            device_id={"head": partner(h, t)}, device_id_type=MESH,
        )

    def when_start(condition, copies):
        @pl.when(condition)
        def _():
            for copy in copies:
                copy.start()

    half = rows // 2
    mine = lax.rem(b, 2) * half
    weight_copies, pair_copies = [], []
    for t in list(range(2, nh)) + [1]:
        to = partner(h, t)
        for m, ref in enumerate((wk_ref, wv_ref)):
            if t == 1:
                src, dst = ref.at[pl.ds(to * rows, rows), :], weights.at[t, m]
            else:
                src = ref.at[pl.ds(to * rows + mine, half), :]
                dst = weights.at[t, m, pl.ds(mine, half), :]
                pair_copies.append(
                    pltpu.make_async_remote_copy(
                        src_ref=dst, dst_ref=dst, send_sem=y_send.at[t, m], recv_sem=y_recv.at[t, m],
                        device_id={"seq": partner(b, 1)}, device_id_type=MESH,
                    )
                )
            copy = across(src, dst, w_send.at[t, m], w_recv.at[t, m], t)
            copy.start()
            weight_copies.append((t, copy))

    def hand_over(first, last):
        for at in range(first, min(last, len(pair_copies))):
            weight_copies[at][1].wait_recv()
            pair_copies[at].start()

    own_copies = []
    for m, ref in enumerate((wk_ref, wv_ref)):
        copy = pltpu.make_async_copy(ref.at[pl.ds(h * rows, rows), :], weights.at[0, m], w_own.at[m])
        copy.start()
        own_copies.append(copy)

    for j in range(tokens // SCALE_BLOCK):
        at = slice(j * SCALE_BLOCK, (j + 1) * SCALE_BLOCK)
        for g in range(heads):
            key_true[at, cols(g)] = (
                k_ref[at, cols(g)].astype(F32) * power_of_two(ke_ref[j, g])
            ).astype(BF16)
    key_far = along(key_true, raw_far, fwd_send.at[0], fwd_recv.at[0], 2)
    when_start(b + 2 < n, [key_far])
    keys_own = key_true[...]
    total_own[...] = jnp.broadcast_to(
        jnp.sum(keys_own.astype(F32), axis=0, keepdims=True), total_own.shape
    )
    sum_near = along(total_own, total_near, fwd_send.at[1], fwd_recv.at[1], 1)
    when_start(b + 1 < n, [sum_near])
    for j in range(tokens // SCALE_BLOCK):
        at = slice(j * SCALE_BLOCK, (j + 1) * SCALE_BLOCK)
        for g in range(heads):
            value[g, own + j * SCALE_BLOCK : own + (j + 1) * SCALE_BLOCK, :] = (
                v_ref[at, cols(g)].astype(F32) * power_of_two(ve_ref[j, g])
            ).astype(BF16)

    def halo(ref, g, kind):
        src = ref.at[g, own : own + tokens]
        at = 2 + 4 * g + 2 * kind
        return (
            along(src, ref.at[g, tokens:own], fwd_send.at[at], fwd_recv.at[at], 1),
            along(src, ref.at[g, 0:tokens], fwd_send.at[at + 1], fwd_recv.at[at + 1], 2),
        )

    halos = [(halo(value, g, 0), halo(smooth, g, 1)) for g in range(heads)]

    def send_halo(copies):
        when_start(b + 2 < n, [copies[1]])
        when_start(b + 1 < n, [copies[0]])

    send_halo(halos[0][0])

    @pl.when(b < 1)
    def _():
        total_near[...] = jnp.zeros_like(total_near)
        for g in range(heads):
            value[g, tokens:own, :] = jnp.zeros((tokens, D), BF16)
            smooth[g, tokens:own, :] = jnp.zeros((tokens, D), BF16)

    @pl.when(b < 2)
    def _():
        raw_far[...] = jnp.zeros_like(raw_far)
        for g in range(heads):
            value[g, 0:tokens, :] = jnp.zeros((tokens, D), BF16)
            smooth[g, 0:tokens, :] = jnp.zeros((tokens, D), BF16)

    row_at = lax.broadcasted_iota(jnp.int32, (tokens, tokens), 0)
    col_at = lax.broadcasted_iota(jnp.int32, (tokens, tokens), 1)
    lower = jnp.where(row_at >= col_at, 1.0, 0.0).astype(BF16)
    running = jnp.dot(lower, keys_own, preferred_element_type=F32)
    place = b * tokens + lax.broadcasted_iota(jnp.int32, (tokens, 1), 0)
    counts = jnp.clip(place + 1, 1, ATTEND_WINDOW).astype(F32)

    @pl.when(b >= 1)
    def _():
        sum_near.wait_recv()

    @pl.when(b >= 2)
    def _():
        key_far.wait_recv()

    far = jnp.dot(lower, raw_far[...], preferred_element_type=F32)
    mean = (running - far + far[tokens - 1 :, :] + total_near[0:1, :]) / counts
    smoothed = (keys_own.astype(F32) - mean).astype(BF16)
    for g in range(heads):
        smooth[g, own : own + tokens, :] = smoothed[:, cols(g)]
    send_halo(halos[0][1])
    for g in range(1, heads):
        send_halo(halos[g][0])
        send_halo(halos[g][1])
    dk[...] = jnp.zeros_like(dk)
    dv[...] = jnp.zeros_like(dv)

    tile = SCALE_BLOCK
    span = ATTEND_WINDOW + tile
    scale = QUERY_SCALE ** (-0.5)
    group = q_ref.shape[1] // (heads * D)
    width = group * tile
    key_row = lax.broadcasted_iota(jnp.int32, (ATTEND_WINDOW, width), 0)
    near_row = lax.broadcasted_iota(jnp.int32, (tile, width), 0)
    lane = lax.rem(lax.broadcasted_iota(jnp.int32, (1, width), 1), tile)

    def far_grad(g, i):
        at = pl.ds(pl.multiple_of(i * tile, tile), tile)
        return along(
            grad_out.at[g, 1, at, :], grad_in.at[g, 1, at, :], far_send.at[g, i], far_recv.at[g, i], -2
        )

    def put_grad(g, d, at, window):
        grad_out[g, d - 1, at, :D] = (dk[g, window, :] * scale).astype(BF16)
        grad_out[g, d - 1, at, D:] = dv[g, window, :].astype(BF16)

    near_copies = []
    for g in range(heads):
        @pl.when(b >= 1)
        def _(g=g):
            for copies in halos[g]:
                copies[0].wait_recv()

        @pl.when(b >= 2)
        def _(g=g):
            for copies in halos[g]:
                copies[1].wait_recv()

        smooth_t[...] = smooth[g].astype(F32).T.astype(BF16)

        def one_tile(i, carry, g=g):
            begin = pl.multiple_of(i * tile, tile)
            at = pl.ds(begin, tile)
            window = pl.ds(begin, span)
            q = jnp.concatenate([q_ref[at, cols(g * group + u)] for u in range(group)], 0)
            do = jnp.concatenate([do_ref[at, cols(g * group + u)] for u in range(group)], 0)
            keys = smooth[g, window, :]
            values = value[g, window, :]
            scores = contract_last(keys, q)
            first = jnp.maximum(lane + 1, (2 - b) * tokens - begin)
            scores = jnp.concatenate(
                [
                    jnp.where(key_row >= first, scores[:ATTEND_WINDOW], -jnp.inf),
                    jnp.where(near_row <= lane, scores[ATTEND_WINDOW:], -jnp.inf),
                ],
                0,
            )
            highest = jnp.max(scores, axis=0, keepdims=True)
            powers = jnp.exp2((scores - highest) * (scale * LOG2_E))
            shares = powers * (1.0 / jnp.sum(powers, axis=0, keepdims=True))
            rounded = shares.astype(BF16)
            share_grad = contract_last(values, do)
            row_dot = jnp.sum(rounded.astype(F32) * share_grad, axis=0, keepdims=True)
            score_grad = (shares * (share_grad - row_dot)).astype(BF16)
            dv[g, window, :] += jnp.dot(rounded, do, preferred_element_type=F32)
            dk[g, window, :] += jnp.dot(score_grad, q, preferred_element_type=F32)
            dq = jnp.dot(smooth_t[:, window], score_grad, preferred_element_type=F32) * scale
            dq = dq.T.astype(BF16)
            for u in range(group):
                dq_ref[at, cols(g * group + u)] = dq[u * tile : (u + 1) * tile]
            put_grad(g, 2, at, at)
            when_start(b >= 2, [far_grad(g, i)])
            return carry

        lax.fori_loop(0, tokens // tile, one_tile, 0)
        put_grad(g, 1, slice(0, tokens), slice(tokens, own))
        copy = along(grad_out.at[g, 0], grad_in.at[g, 0], g_send.at[g], g_recv.at[g], -1)
        when_start(b >= 1, [copy])
        near_copies.append(copy)
        share = -(-len(pair_copies) // heads)
        hand_over(g * share, (g + 1) * share)

    share_copies = []
    onward = []
    for g in range(heads):
        @pl.when(b + 1 < n)
        def _(g=g):
            near_copies[g].wait_recv()

        @pl.when(b + 1 >= n)
        def _(g=g):
            grad_in[g, 0] = jnp.zeros(grad_in.shape[2:], BF16)

        @pl.when(b + 2 < n)
        def _(g=g):
            for i in range(tokens // tile):
                far_grad(g, i).wait_recv()

        @pl.when(b + 2 >= n)
        def _(g=g):
            grad_in[g, 1] = jnp.zeros(grad_in.shape[2:], BF16)

        for j in range(tokens // SCALE_BLOCK):
            at = slice(j * SCALE_BLOCK, (j + 1) * SCALE_BLOCK)
            here = slice(own + j * SCALE_BLOCK, own + (j + 1) * SCALE_BLOCK)
            for m, (ref, exponent, factor) in enumerate(
                ((dk, ke_ref, scale), (dv, ve_ref, 1.0))
            ):
                whole = ref[g, here, :] * factor
                for d in (1, 2):
                    whole = whole + grad_in[g, d - 1, at, cols(m)].astype(F32)
                scaled[g, at, cols(m)] = (whole * power_of_two(exponent[j, g])).astype(BF16)
        for t in list(range(2, nh, 2)) + [1]:
            copy = across(
                scaled.at[g], gathered.at[t - 1, g], s_send.at[t - 1, g], s_recv.at[t - 1, g], t
            )
            copy.start()
            share_copies.append((t, copy))
            if t > 1:
                onward.append(
                    (
                        t,
                        copy,
                        across(
                            gathered.at[t - 1, g], gathered.at[t, g],
                            s_send.at[t, g], s_recv.at[t, g], 1,
                        ),
                    )
                )

    chunk = rows // 4

    def product(t, at):
        total = None
        for g in range(heads):
            left = jnp.concatenate([weights[t, 0, at, cols(g)], weights[t, 1, at, cols(g)]], 1)
            right = scaled[g] if t == 0 else gathered[t - 1, g]
            term = contract_last(left, right)
            total = term if total is None else total + term
        return total

    for copy in own_copies:
        copy.wait()
    for t in range(nh):
        if t == 2:
            for copy in pair_copies:
                copy.wait_recv()
        if t == 1:
            for source, copy in weight_copies:
                if source == 1:
                    copy.wait_recv()
            for source, copy in share_copies:
                if source == 1:
                    copy.wait_recv()
        for source, arrived, copy in onward:
            if source == t:
                arrived.wait_recv()
                copy.start()
            if source == t - 1:
                copy.wait_recv()

        def one_chunk(c, carry, t=t):
            at = pl.ds(pl.multiple_of(c * chunk, 16), chunk)
            total = product(t, at)
            if t > 0:
                total = total + acc[at, :]
            if t < nh - 1:
                acc[at, :] = total
            else:
                out_ref[at, :] = total.astype(BF16)
            return carry

        lax.fori_loop(0, 4, one_chunk, 0)

    @pl.when(b + 1 < n)
    def _():
        sum_near.wait_send()
        for pair in halos:
            for copies in pair:
                copies[0].wait_send()

    @pl.when(b + 2 < n)
    def _():
        key_far.wait_send()
        for pair in halos:
            for copies in pair:
                copies[1].wait_send()

    @pl.when(b >= 1)
    def _():
        for copy in near_copies:
            copy.wait_send()

    @pl.when(b >= 2)
    def _():
        for g in range(heads):
            for i in range(tokens // tile):
                far_grad(g, i).wait_send()

    for _, copy in weight_copies + share_copies:
        copy.wait_send()
    for copy in pair_copies:
        copy.wait_send()
    for _, _, copy in onward:
        copy.wait_send()


def solution(mesh):
    n, nh = mesh.shape["seq"], mesh.shape["head"]

    def local(q, k, v, do, ke, ve, wk, wv):
        tokens, width = k.shape
        heads = width // HEAD_SIZE
        assert ATTEND_WINDOW == 2 * tokens
        rows = wk.shape[0] // nh
        vmem = pl.BlockSpec(memory_space=pltpu.VMEM)
        smem = pl.BlockSpec(memory_space=pltpu.SMEM)
        hbm = pl.BlockSpec(memory_space=pl.ANY)
        dma = pltpu.SemaphoreType.DMA
        return pl.pallas_call(
            functools.partial(kernel, n, nh),
            out_shape=(
                jax.ShapeDtypeStruct(q.shape, BF16),
                jax.ShapeDtypeStruct((rows, tokens), BF16),
            ),
            in_specs=[vmem, vmem, vmem, vmem, smem, smem, hbm, hbm],
            out_specs=(vmem, vmem),
            scratch_shapes=[
                pltpu.VMEM((tokens, width), BF16),
                pltpu.VMEM((tokens, width), BF16),
                pltpu.VMEM((8, width), F32),
                pltpu.VMEM((8, width), F32),
                pltpu.VMEM((heads, 3 * tokens, HEAD_SIZE), BF16),
                pltpu.VMEM((heads, 3 * tokens, HEAD_SIZE), BF16),
                pltpu.VMEM((HEAD_SIZE, 3 * tokens), BF16),
                pltpu.VMEM((heads, 3 * tokens, HEAD_SIZE), F32),
                pltpu.VMEM((heads, 3 * tokens, HEAD_SIZE), F32),
                pltpu.VMEM((heads, 2, tokens, 2 * HEAD_SIZE), BF16),
                pltpu.VMEM((heads, 2, tokens, 2 * HEAD_SIZE), BF16),
                pltpu.VMEM((heads, tokens, 2 * HEAD_SIZE), BF16),
                pltpu.VMEM((nh - 1, heads, tokens, 2 * HEAD_SIZE), BF16),
                pltpu.VMEM((nh, 2, rows, width), BF16),
                pltpu.VMEM((rows, tokens), F32),
                dma((2 + 4 * heads,)), dma((2 + 4 * heads,)),
                dma((nh, 2)), dma((nh, 2)), dma((nh, 2)), dma((nh, 2)), dma((2,)),
                dma((heads,)), dma((heads,)),
                dma((heads, tokens // SCALE_BLOCK)), dma((heads, tokens // SCALE_BLOCK)),
                dma((nh - 1, heads)), dma((nh - 1, heads)),
            ],
            compiler_params=pltpu.CompilerParams(
                collective_id=0, has_side_effects=True, vmem_limit_bytes=56 * 2**20
            ),
        )(q, k, v, do, ke, ve, wk, wv)

    in_specs = (P("seq", "head"),) * 6 + (P(None, "head"),) * 2
    out_specs = (P("seq", "head"), P("head", "seq"))
    return jax.shard_map(local, mesh=mesh, in_specs=in_specs, out_specs=out_specs, check_vma=False)
```

```python
import functools

import jax
import jax.numpy as jnp
from jax import lax
from jax.experimental import pallas as pl
from jax.experimental.pallas import tpu as pltpu
from jax.sharding import PartitionSpec as P

HEAD_SIZE = 128
QUERY_SCALE = 168
ATTEND_WINDOW = 1024
SCALE_BLOCK = 128
LOG2_E = 1.4426950408889634
MESH = pl.DeviceIdType.MESH
F32 = jnp.float32
BF16 = jnp.bfloat16


def power_of_two(exponent):
    return jnp.where(exponent > 0, 2.0, jnp.where(exponent < 0, 0.5, 1.0)).astype(F32)


def contract_last(a, b):
    return lax.dot_general(a, b, (((1,), (1,)), ((), ())), preferred_element_type=F32)


def partner(h, t):
    other, bit = h, 1
    while bit <= t:
        if t & bit:
            other = other + bit - 2 * bit * lax.rem(lax.div(h, bit), 2)
        bit *= 2
    return other


def kernel(
    n, nh, q_ref, k_ref, v_ref, do_ref, ke_ref, ve_ref, wk_ref, wv_ref, dq_ref, out_ref,
    key_true, raw_far, total_own, total_near, smooth, value, smooth_t, dk, dv, grad_out, grad_in,
    scaled, gathered, weights, acc,
    fwd_send, fwd_recv, w_send, w_recv, y_send, y_recv, w_own, g_send, g_recv, far_send, far_recv, s_send, s_recv,
):
    tokens = q_ref.shape[0]
    heads = k_ref.shape[1] // HEAD_SIZE
    D = HEAD_SIZE
    b = lax.axis_index("seq")
    h = lax.axis_index("head")
    rows = out_ref.shape[0]
    own = 2 * tokens

    def cols(g):
        return slice(g * D, (g + 1) * D)

    barrier = pltpu.get_barrier_semaphore()
    for d in (1, 2):
        for to in (lax.rem(b + d, n), lax.rem(b + n - d, n)):
            pl.semaphore_signal(barrier, inc=1, device_id={"seq": to}, device_id_type=MESH)
    for t in range(1, nh):
        pl.semaphore_signal(barrier, inc=1, device_id={"head": partner(h, t)}, device_id_type=MESH)
    pl.semaphore_wait(barrier, 4 + nh - 1)

    def along(src, dst, send, recv, step):
        return pltpu.make_async_remote_copy(
            src_ref=src, dst_ref=dst, send_sem=send, recv_sem=recv,
            device_id={"seq": lax.rem(b + n + step, n)}, device_id_type=MESH,
        )

    def across(src, dst, send, recv, t):
        return pltpu.make_async_remote_copy(
            src_ref=src, dst_ref=dst, send_sem=send, recv_sem=recv,
            device_id={"head": partner(h, t)}, device_id_type=MESH,
        )

    def when_start(condition, copies):
        @pl.when(condition)
        def _():
            for copy in copies:
                copy.start()

    half = rows // 2
    mine = lax.rem(b, 2) * half
    weight_copies, pair_copies = [], []
    for t in list(range(2, nh)) + [1]:
        to = partner(h, t)
        for m, ref in enumerate((wk_ref, wv_ref)):
            if t == 1:
                src, dst = ref.at[pl.ds(to * rows, rows), :], weights.at[t, m]
            else:
                src = ref.at[pl.ds(to * rows + mine, half), :]
                dst = weights.at[t, m, pl.ds(mine, half), :]
                pair_copies.append(
                    pltpu.make_async_remote_copy(
                        src_ref=dst, dst_ref=dst, send_sem=y_send.at[t, m], recv_sem=y_recv.at[t, m],
                        device_id={"seq": partner(b, 1)}, device_id_type=MESH,
                    )
                )
            copy = across(src, dst, w_send.at[t, m], w_recv.at[t, m], t)
            copy.start()
            weight_copies.append((t, copy))

    def hand_over(first, last):
        for at in range(first, min(last, len(pair_copies))):
            weight_copies[at][1].wait_recv()
            pair_copies[at].start()

    own_copies = []
    for m, ref in enumerate((wk_ref, wv_ref)):
        copy = pltpu.make_async_copy(ref.at[pl.ds(h * rows, rows), :], weights.at[0, m], w_own.at[m])
        copy.start()
        own_copies.append(copy)

    for j in range(tokens // SCALE_BLOCK):
        at = slice(j * SCALE_BLOCK, (j + 1) * SCALE_BLOCK)
        for g in range(heads):
            key_true[at, cols(g)] = (
                k_ref[at, cols(g)].astype(F32) * power_of_two(ke_ref[j : j + 1, g : g + 1])
            ).astype(BF16)
    key_far = along(key_true, raw_far, fwd_send.at[0], fwd_recv.at[0], 2)
    when_start(b + 2 < n, [key_far])
    keys_own = key_true[...]
    total_own[...] = jnp.broadcast_to(
        jnp.sum(keys_own.astype(F32), axis=0, keepdims=True), total_own.shape
    )
    sum_near = along(total_own, total_near, fwd_send.at[1], fwd_recv.at[1], 1)
    when_start(b + 1 < n, [sum_near])
    for j in range(tokens // SCALE_BLOCK):
        at = slice(j * SCALE_BLOCK, (j + 1) * SCALE_BLOCK)
        for g in range(heads):
            value[g, own + j * SCALE_BLOCK : own + (j + 1) * SCALE_BLOCK, :] = (
                v_ref[at, cols(g)].astype(F32) * power_of_two(ve_ref[j : j + 1, g : g + 1])
            ).astype(BF16)

    def halo(ref, g, kind):
        src = ref.at[g, own : own + tokens]
        at = 2 + 4 * g + 2 * kind
        return (
            along(src, ref.at[g, tokens:own], fwd_send.at[at], fwd_recv.at[at], 1),
            along(src, ref.at[g, 0:tokens], fwd_send.at[at + 1], fwd_recv.at[at + 1], 2),
            along(ref.at[g, 0:tokens], ref.at[g, tokens:own], fwd_send.at[at], fwd_recv.at[at], -1),
        )

    halos = [(halo(value, g, 0), halo(smooth, g, 1)) for g in range(heads)]

    def send_halo(copies):
        when_start(b + 2 < n, [copies[1]])
        when_start(even, [copies[0]])

    even = lax.rem(b, 2) == 0
    passes_on = jnp.logical_and(lax.rem(b, 2) == 1, b >= 2)
    send_halo(halos[0][0])

    @pl.when(b < 1)
    def _():
        total_near[...] = jnp.zeros_like(total_near)
        for g in range(heads):
            value[g, tokens:own, :] = jnp.zeros((tokens, D), BF16)
            smooth[g, tokens:own, :] = jnp.zeros((tokens, D), BF16)

    @pl.when(b < 2)
    def _():
        raw_far[...] = jnp.zeros_like(raw_far)
        for g in range(heads):
            value[g, 0:tokens, :] = jnp.zeros((tokens, D), BF16)
            smooth[g, 0:tokens, :] = jnp.zeros((tokens, D), BF16)

    row_at = lax.broadcasted_iota(jnp.int32, (tokens, tokens), 0)
    col_at = lax.broadcasted_iota(jnp.int32, (tokens, tokens), 1)
    lower = jnp.where(row_at >= col_at, 1.0, 0.0).astype(BF16)
    running = jnp.dot(lower, keys_own, preferred_element_type=F32)
    place = b * tokens + lax.broadcasted_iota(jnp.int32, (tokens, 1), 0)
    counts = jnp.clip(place + 1, 1, ATTEND_WINDOW).astype(F32)

    @pl.when(b >= 1)
    def _():
        sum_near.wait_recv()

    @pl.when(b >= 2)
    def _():
        key_far.wait_recv()

    far = jnp.dot(lower, raw_far[...], preferred_element_type=F32)
    mean = (running - far + far[tokens - 1 :, :] + total_near[0:1, :]) / counts
    smoothed = (keys_own.astype(F32) - mean).astype(BF16)
    for g in range(heads):
        smooth[g, own : own + tokens, :] = smoothed[:, cols(g)]
    send_halo(halos[0][1])
    for g in range(1, heads):
        send_halo(halos[g][0])
        send_halo(halos[g][1])
    dk[...] = jnp.zeros_like(dk)
    dv[...] = jnp.zeros_like(dv)

    tile = SCALE_BLOCK
    span = ATTEND_WINDOW + tile
    scale = QUERY_SCALE ** (-0.5)
    group = q_ref.shape[1] // (heads * D)
    width = group * tile
    key_row = lax.broadcasted_iota(jnp.int32, (ATTEND_WINDOW, width), 0)
    near_row = lax.broadcasted_iota(jnp.int32, (tile, width), 0)
    lane = lax.rem(lax.broadcasted_iota(jnp.int32, (1, width), 1), tile)

    def far_grad(g, i):
        at = pl.ds(pl.multiple_of(i * tile, tile), tile)
        return along(
            grad_out.at[g, 1, at, :], grad_in.at[g, 1, at, :], far_send.at[g, i], far_recv.at[g, i], -2
        )

    def put_grad(g, d, at, window):
        grad_out[g, d - 1, at, :D] = (dk[g, window, :] * scale).astype(BF16)
        grad_out[g, d - 1, at, D:] = dv[g, window, :].astype(BF16)

    near_copies = []
    for g in range(heads):
        for copies in halos[g]:
            @pl.when(b >= 2)
            def _(copies=copies):
                copies[1].wait_recv()

            when_start(passes_on, [copies[2]])

        @pl.when(b >= 1)
        def _(g=g):
            for copies in halos[g]:
                copies[0].wait_recv()

        smooth_t[...] = smooth[g].astype(F32).T.astype(BF16)

        def one_tile(i, carry, g=g):
            begin = pl.multiple_of(i * tile, tile)
            at = pl.ds(begin, tile)
            window = pl.ds(begin, span)
            q = jnp.concatenate([q_ref[at, cols(g * group + u)] for u in range(group)], 0)
            do = jnp.concatenate([do_ref[at, cols(g * group + u)] for u in range(group)], 0)
            keys = smooth[g, window, :]
            values = value[g, window, :]
            scores = contract_last(keys, q)
            first = jnp.maximum(lane + 1, (2 - b) * tokens - begin)
            scores = jnp.concatenate(
                [
                    jnp.where(key_row >= first, scores[:ATTEND_WINDOW], -jnp.inf),
                    jnp.where(near_row <= lane, scores[ATTEND_WINDOW:], -jnp.inf),
                ],
                0,
            )
            highest = jnp.max(scores, axis=0, keepdims=True)
            powers = jnp.exp2((scores - highest) * (scale * LOG2_E))
            shares = powers * (1.0 / jnp.sum(powers, axis=0, keepdims=True))
            rounded = shares.astype(BF16)
            share_grad = contract_last(values, do)
            row_dot = jnp.sum(rounded.astype(F32) * share_grad, axis=0, keepdims=True)
            score_grad = (shares * (share_grad - row_dot)).astype(BF16)
            dv[g, window, :] += jnp.dot(rounded, do, preferred_element_type=F32)
            dk[g, window, :] += jnp.dot(score_grad, q, preferred_element_type=F32)
            dq = jnp.dot(smooth_t[:, window], score_grad, preferred_element_type=F32) * scale
            dq = dq.T.astype(BF16)
            for u in range(group):
                dq_ref[at, cols(g * group + u)] = dq[u * tile : (u + 1) * tile]
            put_grad(g, 2, at, at)
            when_start(b >= 2, [far_grad(g, i)])
            return carry

        lax.fori_loop(0, tokens // tile, one_tile, 0)
        put_grad(g, 1, slice(0, tokens), slice(tokens, own))
        copy = along(grad_out.at[g, 0], grad_in.at[g, 0], g_send.at[g], g_recv.at[g], -1)
        when_start(b >= 1, [copy])
        near_copies.append(copy)
        share = -(-len(pair_copies) // heads)
        hand_over(g * share, (g + 1) * share)

    share_copies = []
    onward = []
    for g in range(heads):
        @pl.when(b + 1 < n)
        def _(g=g):
            near_copies[g].wait_recv()

        @pl.when(b + 1 >= n)
        def _(g=g):
            grad_in[g, 0] = jnp.zeros(grad_in.shape[2:], BF16)

        @pl.when(b + 2 < n)
        def _(g=g):
            for i in range(tokens // tile):
                far_grad(g, i).wait_recv()

        @pl.when(b + 2 >= n)
        def _(g=g):
            grad_in[g, 1] = jnp.zeros(grad_in.shape[2:], BF16)

        for j in range(tokens // SCALE_BLOCK):
            at = slice(j * SCALE_BLOCK, (j + 1) * SCALE_BLOCK)
            here = slice(own + j * SCALE_BLOCK, own + (j + 1) * SCALE_BLOCK)
            for m, (ref, exponent, factor) in enumerate(
                ((dk, ke_ref, scale), (dv, ve_ref, 1.0))
            ):
                whole = ref[g, here, :] * factor
                for d in (1, 2):
                    whole = whole + grad_in[g, d - 1, at, cols(m)].astype(F32)
                scaled[g, at, cols(m)] = (whole * power_of_two(exponent[j : j + 1, g : g + 1])).astype(BF16)
        for t in list(range(2, nh, 2)) + [1]:
            copy = across(
                scaled.at[g], gathered.at[t - 1, g], s_send.at[t - 1, g], s_recv.at[t - 1, g], t
            )
            copy.start()
            share_copies.append((t, copy))
            if t > 1:
                onward.append(
                    (
                        t,
                        copy,
                        across(
                            gathered.at[t - 1, g], gathered.at[t, g],
                            s_send.at[t, g], s_recv.at[t, g], 1,
                        ),
                    )
                )

    chunk = rows // 4

    def product(t, at):
        total = None
        for g in range(heads):
            left = jnp.concatenate([weights[t, 0, at, cols(g)], weights[t, 1, at, cols(g)]], 1)
            right = scaled[g] if t == 0 else gathered[t - 1, g]
            term = contract_last(left, right)
            total = term if total is None else total + term
        return total

    for copy in own_copies:
        copy.wait()
    for t in range(nh):
        if t == 2:
            for copy in pair_copies:
                copy.wait_recv()
        if t == 1:
            for source, copy in weight_copies:
                if source == 1:
                    copy.wait_recv()
            for source, copy in share_copies:
                if source == 1:
                    copy.wait_recv()
        for source, arrived, copy in onward:
            if source == t:
                arrived.wait_recv()
                copy.start()
            if source == t - 1:
                copy.wait_recv()

        def one_chunk(c, carry, t=t):
            at = pl.ds(pl.multiple_of(c * chunk, 16), chunk)
            total = product(t, at)
            if t > 0:
                total = total + acc[at, :]
            if t < nh - 1:
                acc[at, :] = total
            else:
                out_ref[at, :] = total.astype(BF16)
            return carry

        lax.fori_loop(0, 4, one_chunk, 0)

    @pl.when(b + 1 < n)
    def _():
        sum_near.wait_send()

    @pl.when(even)
    def _():
        for pair in halos:
            for copies in pair:
                copies[0].wait_send()

    @pl.when(passes_on)
    def _():
        for pair in halos:
            for copies in pair:
                copies[2].wait_send()

    @pl.when(b + 2 < n)
    def _():
        key_far.wait_send()
        for pair in halos:
            for copies in pair:
                copies[1].wait_send()

    @pl.when(b >= 1)
    def _():
        for copy in near_copies:
            copy.wait_send()

    @pl.when(b >= 2)
    def _():
        for g in range(heads):
            for i in range(tokens // tile):
                far_grad(g, i).wait_send()

    for _, copy in weight_copies + share_copies:
        copy.wait_send()
    for copy in pair_copies:
        copy.wait_send()
    for _, _, copy in onward:
        copy.wait_send()


def solution(mesh):
    n, nh = mesh.shape["seq"], mesh.shape["head"]

    def local(q, k, v, do, ke, ve, wk, wv):
        tokens, width = k.shape
        heads = width // HEAD_SIZE
        assert ATTEND_WINDOW == 2 * tokens and n % 2 == 0
        rows = wk.shape[0] // nh
        vmem = pl.BlockSpec(memory_space=pltpu.VMEM)
        hbm = pl.BlockSpec(memory_space=pl.ANY)
        dma = pltpu.SemaphoreType.DMA
        return pl.pallas_call(
            functools.partial(kernel, n, nh),
            out_shape=(
                jax.ShapeDtypeStruct(q.shape, BF16),
                jax.ShapeDtypeStruct((rows, tokens), BF16),
            ),
            in_specs=[vmem, vmem, vmem, vmem, vmem, vmem, hbm, hbm],
            out_specs=(vmem, vmem),
            scratch_shapes=[
                pltpu.VMEM((tokens, width), BF16),
                pltpu.VMEM((tokens, width), BF16),
                pltpu.VMEM((8, width), F32),
                pltpu.VMEM((8, width), F32),
                pltpu.VMEM((heads, 3 * tokens, HEAD_SIZE), BF16),
                pltpu.VMEM((heads, 3 * tokens, HEAD_SIZE), BF16),
                pltpu.VMEM((HEAD_SIZE, 3 * tokens), BF16),
                pltpu.VMEM((heads, 3 * tokens, HEAD_SIZE), F32),
                pltpu.VMEM((heads, 3 * tokens, HEAD_SIZE), F32),
                pltpu.VMEM((heads, 2, tokens, 2 * HEAD_SIZE), BF16),
                pltpu.VMEM((heads, 2, tokens, 2 * HEAD_SIZE), BF16),
                pltpu.VMEM((heads, tokens, 2 * HEAD_SIZE), BF16),
                pltpu.VMEM((nh - 1, heads, tokens, 2 * HEAD_SIZE), BF16),
                pltpu.VMEM((nh, 2, rows, width), BF16),
                pltpu.VMEM((rows, tokens), F32),
                dma((2 + 4 * heads,)), dma((2 + 4 * heads,)),
                dma((nh, 2)), dma((nh, 2)), dma((nh, 2)), dma((nh, 2)), dma((2,)),
                dma((heads,)), dma((heads,)),
                dma((heads, tokens // SCALE_BLOCK)), dma((heads, tokens // SCALE_BLOCK)),
                dma((nh - 1, heads)), dma((nh - 1, heads)),
            ],
            compiler_params=pltpu.CompilerParams(
                collective_id=0, has_side_effects=True, vmem_limit_bytes=56 * 2**20
            ),
        )(q, k, v, do, ke, ve, wk, wv)

    in_specs = (P("seq", "head"),) * 6 + (P(None, "head"),) * 2
    out_specs = (P("seq", "head"), P("head", "seq"))
    return jax.shard_map(local, mesh=mesh, in_specs=in_specs, out_specs=out_specs, check_vma=False)
```

```python
import functools

import jax
import jax.numpy as jnp
from jax import lax
from jax.experimental import pallas as pl
from jax.experimental.pallas import tpu as pltpu
from jax.sharding import PartitionSpec as P

HEAD_SIZE = 128
QUERY_SCALE = 168
ATTEND_WINDOW = 1024
SCALE_BLOCK = 128
LOG2_E = 1.4426950408889634
MESH = pl.DeviceIdType.MESH
F32 = jnp.float32
BF16 = jnp.bfloat16


def power_of_two(exponent):
    return jnp.where(exponent > 0, 2.0, jnp.where(exponent < 0, 0.5, 1.0)).astype(F32)


def contract_last(a, b):
    return lax.dot_general(a, b, (((1,), (1,)), ((), ())), preferred_element_type=F32)


def partner(h, t):
    other, bit = h, 1
    while bit <= t:
        if t & bit:
            other = other + bit - 2 * bit * lax.rem(lax.div(h, bit), 2)
        bit *= 2
    return other


def kernel(
    n, nh, q_ref, k_ref, v_ref, do_ref, ke_ref, ve_ref, wk_ref, wv_ref, dq_ref, out_ref,
    key_true, raw_far, total_own, total_near, smooth, value, smooth_t, dk, dv, grad_out, grad_in,
    scaled, gathered, weights, acc,
    fwd_send, fwd_recv, w_send, w_recv, y_send, y_recv, w_own, g_send, g_recv, far_send, far_recv, s_send, s_recv,
):
    tokens = q_ref.shape[0]
    heads = k_ref.shape[1] // HEAD_SIZE
    D = HEAD_SIZE
    b = lax.axis_index("seq")
    h = lax.axis_index("head")
    rows = out_ref.shape[0]
    own = 2 * tokens

    def cols(g):
        return slice(g * D, (g + 1) * D)

    barrier = pltpu.get_barrier_semaphore()
    for d in (1, 2):
        for to in (lax.rem(b + d, n), lax.rem(b + n - d, n)):
            pl.semaphore_signal(barrier, inc=1, device_id={"seq": to}, device_id_type=MESH)
    for t in range(1, nh):
        pl.semaphore_signal(barrier, inc=1, device_id={"head": partner(h, t)}, device_id_type=MESH)
    pl.semaphore_wait(barrier, 4 + nh - 1)

    def along(src, dst, send, recv, step):
        return pltpu.make_async_remote_copy(
            src_ref=src, dst_ref=dst, send_sem=send, recv_sem=recv,
            device_id={"seq": lax.rem(b + n + step, n)}, device_id_type=MESH,
        )

    def across(src, dst, send, recv, t):
        return pltpu.make_async_remote_copy(
            src_ref=src, dst_ref=dst, send_sem=send, recv_sem=recv,
            device_id={"head": partner(h, t)}, device_id_type=MESH,
        )

    def when_start(condition, copies):
        @pl.when(condition)
        def _():
            for copy in copies:
                copy.start()

    half = rows // 2
    mine = lax.rem(b, 2) * half
    weight_copies, pair_copies = [], []
    for t in list(range(nh - 1, 0, -1)):
        to = partner(h, t)
        for m, ref in enumerate((wk_ref, wv_ref)):
            if t < 3:
                src, dst = ref.at[pl.ds(to * rows, rows), :], weights.at[t, m]
            else:
                src = ref.at[pl.ds(to * rows + mine, half), :]
                dst = weights.at[t, m, pl.ds(mine, half), :]
                pair_copies.append(
                    pltpu.make_async_remote_copy(
                        src_ref=dst, dst_ref=dst, send_sem=y_send.at[t, m], recv_sem=y_recv.at[t, m],
                        device_id={"seq": partner(b, 1)}, device_id_type=MESH,
                    )
                )
            copy = across(src, dst, w_send.at[t, m], w_recv.at[t, m], t)
            copy.start()
            weight_copies.append((t, copy))

    def hand_over(first, last):
        for at in range(first, min(last, len(pair_copies))):
            weight_copies[at][1].wait_recv()
            pair_copies[at].start()

    own_copies = []
    for m, ref in enumerate((wk_ref, wv_ref)):
        copy = pltpu.make_async_copy(ref.at[pl.ds(h * rows, rows), :], weights.at[0, m], w_own.at[m])
        copy.start()
        own_copies.append(copy)

    for j in range(tokens // SCALE_BLOCK):
        at = slice(j * SCALE_BLOCK, (j + 1) * SCALE_BLOCK)
        for g in range(heads):
            key_true[at, cols(g)] = (
                k_ref[at, cols(g)].astype(F32) * power_of_two(ke_ref[j : j + 1, g : g + 1])
            ).astype(BF16)
    key_far = along(key_true, raw_far, fwd_send.at[0], fwd_recv.at[0], 2)
    when_start(b + 2 < n, [key_far])
    keys_own = key_true[...]
    total_own[...] = jnp.broadcast_to(
        jnp.sum(keys_own.astype(F32), axis=0, keepdims=True), total_own.shape
    )
    sum_near = along(total_own, total_near, fwd_send.at[1], fwd_recv.at[1], 1)
    when_start(b + 1 < n, [sum_near])
    for j in range(tokens // SCALE_BLOCK):
        at = slice(j * SCALE_BLOCK, (j + 1) * SCALE_BLOCK)
        for g in range(heads):
            value[g, own + j * SCALE_BLOCK : own + (j + 1) * SCALE_BLOCK, :] = (
                v_ref[at, cols(g)].astype(F32) * power_of_two(ve_ref[j : j + 1, g : g + 1])
            ).astype(BF16)

    def halo(ref, g, kind):
        src = ref.at[g, own : own + tokens]
        at = 2 + 4 * g + 2 * kind
        return (
            along(src, ref.at[g, tokens:own], fwd_send.at[at], fwd_recv.at[at], 1),
            along(src, ref.at[g, 0:tokens], fwd_send.at[at + 1], fwd_recv.at[at + 1], 2),
        )

    halos = [(halo(value, g, 0), halo(smooth, g, 1)) for g in range(heads)]

    def send_halo(copies):
        when_start(b + 2 < n, [copies[1]])
        when_start(b + 1 < n, [copies[0]])

    send_halo(halos[0][0])

    @pl.when(b < 1)
    def _():
        total_near[...] = jnp.zeros_like(total_near)
        for g in range(heads):
            value[g, tokens:own, :] = jnp.zeros((tokens, D), BF16)
            smooth[g, tokens:own, :] = jnp.zeros((tokens, D), BF16)

    @pl.when(b < 2)
    def _():
        raw_far[...] = jnp.zeros_like(raw_far)
        for g in range(heads):
            value[g, 0:tokens, :] = jnp.zeros((tokens, D), BF16)
            smooth[g, 0:tokens, :] = jnp.zeros((tokens, D), BF16)

    row_at = lax.broadcasted_iota(jnp.int32, (tokens, tokens), 0)
    col_at = lax.broadcasted_iota(jnp.int32, (tokens, tokens), 1)
    lower = jnp.where(row_at >= col_at, 1.0, 0.0).astype(BF16)
    running = jnp.dot(lower, keys_own, preferred_element_type=F32)
    place = b * tokens + lax.broadcasted_iota(jnp.int32, (tokens, 1), 0)
    counts = jnp.clip(place + 1, 1, ATTEND_WINDOW).astype(F32)

    @pl.when(b >= 1)
    def _():
        sum_near.wait_recv()

    @pl.when(b >= 2)
    def _():
        key_far.wait_recv()

    far = jnp.dot(lower, raw_far[...], preferred_element_type=F32)
    mean = (running - far + far[tokens - 1 :, :] + total_near[0:1, :]) / counts
    smoothed = (keys_own.astype(F32) - mean).astype(BF16)
    for g in range(heads):
        smooth[g, own : own + tokens, :] = smoothed[:, cols(g)]
    send_halo(halos[0][1])
    for g in range(1, heads):
        send_halo(halos[g][0])
        send_halo(halos[g][1])
    dk[...] = jnp.zeros_like(dk)
    dv[...] = jnp.zeros_like(dv)

    tile = SCALE_BLOCK
    span = ATTEND_WINDOW + tile
    scale = QUERY_SCALE ** (-0.5)
    group = q_ref.shape[1] // (heads * D)
    width = group * tile
    key_row = lax.broadcasted_iota(jnp.int32, (ATTEND_WINDOW, width), 0)
    near_row = lax.broadcasted_iota(jnp.int32, (tile, width), 0)
    lane = lax.rem(lax.broadcasted_iota(jnp.int32, (1, width), 1), tile)

    def far_grad(g, i):
        at = pl.ds(pl.multiple_of(i * tile, tile), tile)
        return along(
            grad_out.at[g, 1, at, :], grad_in.at[g, 1, at, :], far_send.at[g, i], far_recv.at[g, i], -2
        )

    def put_grad(g, d, at, window):
        grad_out[g, d - 1, at, :D] = (dk[g, window, :] * scale).astype(BF16)
        grad_out[g, d - 1, at, D:] = dv[g, window, :].astype(BF16)

    near_copies = []
    for g in range(heads):
        @pl.when(b >= 1)
        def _(g=g):
            for copies in halos[g]:
                copies[0].wait_recv()

        @pl.when(b >= 2)
        def _(g=g):
            for copies in halos[g]:
                copies[1].wait_recv()

        if g == 0:
            hand_over(0, len(pair_copies))
        smooth_t[...] = smooth[g].astype(F32).T.astype(BF16)

        def one_tile(i, carry, g=g):
            begin = pl.multiple_of(i * tile, tile)
            at = pl.ds(begin, tile)
            window = pl.ds(begin, span)
            q = jnp.concatenate([q_ref[at, cols(g * group + u)] for u in range(group)], 0)
            do = jnp.concatenate([do_ref[at, cols(g * group + u)] for u in range(group)], 0)
            keys = smooth[g, window, :]
            values = value[g, window, :]
            scores = contract_last(keys, q)
            first = jnp.maximum(lane + 1, (2 - b) * tokens - begin)
            scores = jnp.concatenate(
                [
                    jnp.where(key_row >= first, scores[:ATTEND_WINDOW], -jnp.inf),
                    jnp.where(near_row <= lane, scores[ATTEND_WINDOW:], -jnp.inf),
                ],
                0,
            )
            highest = jnp.max(scores, axis=0, keepdims=True)
            powers = jnp.exp2((scores - highest) * (scale * LOG2_E))
            shares = powers * (1.0 / jnp.sum(powers, axis=0, keepdims=True))
            rounded = shares.astype(BF16)
            share_grad = contract_last(values, do)
            row_dot = jnp.sum(rounded.astype(F32) * share_grad, axis=0, keepdims=True)
            score_grad = (shares * (share_grad - row_dot)).astype(BF16)
            dv[g, window, :] += jnp.dot(rounded, do, preferred_element_type=F32)
            dk[g, window, :] += jnp.dot(score_grad, q, preferred_element_type=F32)
            dq = jnp.dot(smooth_t[:, window], score_grad, preferred_element_type=F32) * scale
            dq = dq.T.astype(BF16)
            for u in range(group):
                dq_ref[at, cols(g * group + u)] = dq[u * tile : (u + 1) * tile]
            put_grad(g, 2, at, at)
            when_start(b >= 2, [far_grad(g, i)])
            return carry

        lax.fori_loop(0, tokens // tile, one_tile, 0)
        put_grad(g, 1, slice(0, tokens), slice(tokens, own))
        copy = along(grad_out.at[g, 0], grad_in.at[g, 0], g_send.at[g], g_recv.at[g], -1)
        when_start(b >= 1, [copy])
        near_copies.append(copy)

    share_copies = []
    onward = []
    for g in range(heads):
        @pl.when(b + 1 < n)
        def _(g=g):
            near_copies[g].wait_recv()

        @pl.when(b + 1 >= n)
        def _(g=g):
            grad_in[g, 0] = jnp.zeros(grad_in.shape[2:], BF16)

        @pl.when(b + 2 < n)
        def _(g=g):
            for i in range(tokens // tile):
                far_grad(g, i).wait_recv()

        @pl.when(b + 2 >= n)
        def _(g=g):
            grad_in[g, 1] = jnp.zeros(grad_in.shape[2:], BF16)

        for j in range(tokens // SCALE_BLOCK):
            at = slice(j * SCALE_BLOCK, (j + 1) * SCALE_BLOCK)
            here = slice(own + j * SCALE_BLOCK, own + (j + 1) * SCALE_BLOCK)
            for m, (ref, exponent, factor) in enumerate(
                ((dk, ke_ref, scale), (dv, ve_ref, 1.0))
            ):
                whole = ref[g, here, :] * factor
                for d in (1, 2):
                    whole = whole + grad_in[g, d - 1, at, cols(m)].astype(F32)
                scaled[g, at, cols(m)] = (whole * power_of_two(exponent[j : j + 1, g : g + 1])).astype(BF16)
        for t in list(range(2, nh, 2)) + [1]:
            copy = across(
                scaled.at[g], gathered.at[t - 1, g], s_send.at[t - 1, g], s_recv.at[t - 1, g], t
            )
            copy.start()
            share_copies.append((t, copy))
            if t > 1:
                onward.append(
                    (
                        t,
                        copy,
                        across(
                            gathered.at[t - 1, g], gathered.at[t, g],
                            s_send.at[t, g], s_recv.at[t, g], 1,
                        ),
                    )
                )

    chunk = rows // 4

    def product(t, at):
        total = None
        for g in range(heads):
            left = jnp.concatenate([weights[t, 0, at, cols(g)], weights[t, 1, at, cols(g)]], 1)
            right = scaled[g] if t == 0 else gathered[t - 1, g]
            term = contract_last(left, right)
            total = term if total is None else total + term
        return total

    for copy in own_copies:
        copy.wait()
    for t in range(nh):
        if t == 3:
            for copy in pair_copies:
                copy.wait_recv()
        if t in (1, 2):
            for source, copy in weight_copies:
                if source == t:
                    copy.wait_recv()
        if t == 1:
            for source, copy in share_copies:
                if source == 1:
                    copy.wait_recv()
        for source, arrived, copy in onward:
            if source == t:
                arrived.wait_recv()
                copy.start()
            if source == t - 1:
                copy.wait_recv()

        def one_chunk(c, carry, t=t):
            at = pl.ds(pl.multiple_of(c * chunk, 16), chunk)
            total = product(t, at)
            if t > 0:
                total = total + acc[at, :]
            if t < nh - 1:
                acc[at, :] = total
            else:
                out_ref[at, :] = total.astype(BF16)
            return carry

        lax.fori_loop(0, 4, one_chunk, 0)

    @pl.when(b + 1 < n)
    def _():
        sum_near.wait_send()
        for pair in halos:
            for copies in pair:
                copies[0].wait_send()

    @pl.when(b + 2 < n)
    def _():
        key_far.wait_send()
        for pair in halos:
            for copies in pair:
                copies[1].wait_send()

    @pl.when(b >= 1)
    def _():
        for copy in near_copies:
            copy.wait_send()

    @pl.when(b >= 2)
    def _():
        for g in range(heads):
            for i in range(tokens // tile):
                far_grad(g, i).wait_send()

    for _, copy in weight_copies + share_copies:
        copy.wait_send()
    for copy in pair_copies:
        copy.wait_send()
    for _, _, copy in onward:
        copy.wait_send()


def solution(mesh):
    n, nh = mesh.shape["seq"], mesh.shape["head"]

    def local(q, k, v, do, ke, ve, wk, wv):
        tokens, width = k.shape
        heads = width // HEAD_SIZE
        assert ATTEND_WINDOW == 2 * tokens
        rows = wk.shape[0] // nh
        vmem = pl.BlockSpec(memory_space=pltpu.VMEM)
        hbm = pl.BlockSpec(memory_space=pl.ANY)
        dma = pltpu.SemaphoreType.DMA
        return pl.pallas_call(
            functools.partial(kernel, n, nh),
            out_shape=(
                jax.ShapeDtypeStruct(q.shape, BF16),
                jax.ShapeDtypeStruct((rows, tokens), BF16),
            ),
            in_specs=[vmem, vmem, vmem, vmem, vmem, vmem, hbm, hbm],
            out_specs=(vmem, vmem),
            scratch_shapes=[
                pltpu.VMEM((tokens, width), BF16),
                pltpu.VMEM((tokens, width), BF16),
                pltpu.VMEM((8, width), F32),
                pltpu.VMEM((8, width), F32),
                pltpu.VMEM((heads, 3 * tokens, HEAD_SIZE), BF16),
                pltpu.VMEM((heads, 3 * tokens, HEAD_SIZE), BF16),
                pltpu.VMEM((HEAD_SIZE, 3 * tokens), BF16),
                pltpu.VMEM((heads, 3 * tokens, HEAD_SIZE), F32),
                pltpu.VMEM((heads, 3 * tokens, HEAD_SIZE), F32),
                pltpu.VMEM((heads, 2, tokens, 2 * HEAD_SIZE), BF16),
                pltpu.VMEM((heads, 2, tokens, 2 * HEAD_SIZE), BF16),
                pltpu.VMEM((heads, tokens, 2 * HEAD_SIZE), BF16),
                pltpu.VMEM((nh - 1, heads, tokens, 2 * HEAD_SIZE), BF16),
                pltpu.VMEM((nh, 2, rows, width), BF16),
                pltpu.VMEM((rows, tokens), F32),
                dma((2 + 4 * heads,)), dma((2 + 4 * heads,)),
                dma((nh, 2)), dma((nh, 2)), dma((nh, 2)), dma((nh, 2)), dma((2,)),
                dma((heads,)), dma((heads,)),
                dma((heads, tokens // SCALE_BLOCK)), dma((heads, tokens // SCALE_BLOCK)),
                dma((nh - 1, heads)), dma((nh - 1, heads)),
            ],
            compiler_params=pltpu.CompilerParams(
                collective_id=0, has_side_effects=True, vmem_limit_bytes=56 * 2**20
            ),
        )(q, k, v, do, ke, ve, wk, wv)

    in_specs = (P("seq", "head"),) * 6 + (P(None, "head"),) * 2
    out_specs = (P("seq", "head"), P("head", "seq"))
    return jax.shard_map(local, mesh=mesh, in_specs=in_specs, out_specs=out_specs, check_vma=False)
```
